768 devices in a mesh: span: 96 (over z, x, core), chord: 8 (over y).
Axes of the slice: x: 4, y: 8, z: 12, core: 2. Of those that a mesh axis runs over, the one named last changes fastest.
Arguments:
- displacement: bfloat16 [96, 8, 1024, 128], P('span', 'chord'), may hold values from -12 to 12
- packed_blocks: bfloat16 [96, 8, 1024, 1024], P('span', 'chord'), as said below
- flex_scale: float32 [96, 8, 1024], P('span', 'chord'), may hold values from 0.5 to 2
- dirichlet_scale: float32 [96, 8, 1024], P('span', 'chord'), may hold values from 0.5 to 2
- dirichlet_diag: bfloat16 [96, 8, 1024], P('span', 'chord'), may hold values from 1.1953125 to 2.5
- link_rows: int32 [96, 8, 4, 256], P('span', 'chord'), may hold values from 0 to 1023, as said below
- link_signs: int32 [96, 8, 4, 256], P('span', 'chord'), may hold values from -1 to 1, as said below
- link_counts: int32 [96, 8, 4], P('span', 'chord'), may hold values from 0 to 256, as said below
Outputs:
- multipliers: float32 [96, 8, 1024, 128], P('span', 'chord')
- residual: float32 [96, 8, 1024, 128], P('span', 'chord')
The draws below stay inside these ranges and needn't reach their ends.
Inputs may be any that keep to these rules, and one draw needn't show every extreme that they name: `link_rows`: for each subdomain the 4 x 256 entries name every row 0 to 1023 exactly once. `link_counts`: each count equals the count of the opposite direction on the neighbour's side; it is 0 at the edges of the mesh and toward unlisted neighbours, otherwise at least 64; some subdomain uses all 256 slots toward a span neighbour and some toward a chord neighbour. `link_signs`: every entry is 1 or -1; slot p toward a neighbour holds the opposite sign of slot p of the opposite direction on that neighbour. `packed_blocks`: each block's diagonal lies between 1.2 and 2.5.
All inputs are finite; a program needn't handle non-finite values.
Results may differ from the reference program's by a relative error of at most 0.0065.
Values may be sent and summed in bfloat16 or wider, within the bound.
No kernel may reach another device: no remote copies, remote signals or barrier semaphores. Data moves between devices by JAX's collectives and lax.ppermute only.
A program may use at most 32 MiB of HBM per device.

```python
import math
import jax
import jax.numpy as jnp
from jax import lax

SUBS_SPAN = 96
SUBS_CHORD = 8
ROWS = 1024
LOADS = 128
SLOTS = 256
ITERS = 1


def link_tables(key):
    base = jax.random.fold_in(key, 4242)
    keys = jax.random.split(base, 7)
    shape2 = (SUBS_SPAN, SUBS_CHORD)
    span_ids = jnp.arange(SUBS_SPAN)[:, None]
    chord_ids = jnp.arange(SUBS_CHORD)[None, :]
    span_count = jax.random.randint(keys[0], shape2, SLOTS // 4, SLOTS + 1)
    span_count = jnp.where(jax.random.randint(keys[1], shape2, 0, 8) > 0, span_count, 0)
    span_count = span_count.at[0, 0].set(SLOTS)
    span_count = jnp.where(span_ids < SUBS_SPAN - 1, span_count, 0)
    chord_count = jax.random.randint(keys[2], shape2, SLOTS // 4, SLOTS + 1)
    chord_count = jnp.where(jax.random.randint(keys[3], shape2, 0, 8) > 0, chord_count, 0)
    chord_count = chord_count.at[0, 0].set(SLOTS)
    chord_count = jnp.where(chord_ids < SUBS_CHORD - 1, chord_count, 0)
    lower_span = jnp.concatenate([jnp.zeros((1, SUBS_CHORD), span_count.dtype), span_count[:-1]], axis=0)
    lower_chord = jnp.concatenate([jnp.zeros((SUBS_SPAN, 1), chord_count.dtype), chord_count[:, :-1]], axis=1)
    counts = jnp.stack([lower_span, span_count, lower_chord, chord_count], axis=-1).astype(jnp.int32)
    perm_keys = jax.random.split(keys[4], SUBS_SPAN * SUBS_CHORD)
    rows = jax.vmap(lambda k: jax.random.permutation(k, ROWS))(perm_keys)
    rows = rows.reshape(SUBS_SPAN, SUBS_CHORD, 4, SLOTS).astype(jnp.int32)
    span_sign = 2 * jax.random.randint(keys[5], (SUBS_SPAN, SUBS_CHORD, SLOTS), 0, 2) - 1
    chord_sign = 2 * jax.random.randint(keys[6], (SUBS_SPAN, SUBS_CHORD, SLOTS), 0, 2) - 1
    lower_span_sign = -jnp.roll(span_sign, 1, axis=0)
    lower_chord_sign = -jnp.roll(chord_sign, 1, axis=1)
    signs = jnp.stack([lower_span_sign, span_sign, lower_chord_sign, chord_sign], axis=2).astype(jnp.int32)
    return (rows, signs, counts)


def draw_link_rows(key, part):
    return link_tables(key)[0]


def draw_link_signs(key, part):
    return link_tables(key)[1]


def draw_link_counts(key, part):
    return link_tables(key)[2]


def draw_packed_blocks(key, part):
    keys = jax.random.split(jax.random.fold_in(key, 17), 2)
    shape = (SUBS_SPAN, SUBS_CHORD, ROWS, ROWS)
    spread = 0.4 / math.sqrt(ROWS)
    off = jax.random.normal(keys[0], shape, jnp.float32) * spread
    diag = jax.random.uniform(keys[1], (SUBS_SPAN, SUBS_CHORD, ROWS), jnp.float32, 1.2, 2.5)
    same = jnp.arange(ROWS)[:, None] == jnp.arange(ROWS)[None, :]
    return jnp.where(same, diag[..., :, None], off).astype(jnp.bfloat16)


def draw_displacement(key, part):
    keys = jax.random.split(jax.random.fold_in(key, 29), 1)
    shape = (SUBS_SPAN, SUBS_CHORD, ROWS, LOADS)
    ramp = (1.0 + 2.0 * jnp.arange(SUBS_SPAN, dtype=jnp.float32) / max(SUBS_SPAN - 1, 1)).reshape(SUBS_SPAN, 1, 1, 1)
    values = jax.random.normal(keys[0], shape, jnp.float32) * ramp
    return jnp.clip(values, -12.0, 12.0).astype(jnp.bfloat16)


def shard_levels(stream_key, extent, cuts, smallest, top_value):
    def one(position, shards_of):
        draws = jax.random.uniform(jax.random.fold_in(jax.random.fold_in(stream_key, 6), position), (shards_of,), jnp.float32, smallest / len(cuts), top_value / len(cuts))
        return jnp.repeat(jnp.exp(draws), extent[position] // shards_of).reshape((-1,) + (1,) * (len(extent) - position - 1))

    level = one(*cuts[0])
    for cut in cuts[1:]:
        level = level * one(*cut)
    return level


def setup_inputs(seed: int = 0) -> dict:
    key_list = jax.random.split(jax.random.key(seed), 9)
    return {
        "displacement": draw_displacement(jax.random.fold_in(key_list[8], 71), 0),
        "packed_blocks": draw_packed_blocks(jax.random.fold_in(key_list[8], 71), 0),
        "flex_scale": jnp.clip(jnp.exp(math.log(2.0) - 1.3862944 * jax.random.uniform(key_list[2], (SUBS_SPAN, SUBS_CHORD, ROWS), jnp.float32) ** shard_levels(key_list[2], (SUBS_SPAN, SUBS_CHORD, ROWS), ((0, 96), (1, 8)), -0.2, 0.2)), 0.5, 2.0),
        "dirichlet_scale": jnp.clip(jnp.exp(math.log(2.0) - 1.3862944 * jax.random.uniform(key_list[3], (SUBS_SPAN, SUBS_CHORD, ROWS), jnp.float32) ** shard_levels(key_list[3], (SUBS_SPAN, SUBS_CHORD, ROWS), ((0, 96), (1, 8)), -0.2, 0.2)), 0.5, 2.0),
        "dirichlet_diag": jnp.clip(1.1953125 + 1.3046875 * jax.random.uniform(key_list[4], (SUBS_SPAN, SUBS_CHORD, ROWS), jnp.float32) ** shard_levels(key_list[4], (SUBS_SPAN, SUBS_CHORD, ROWS), ((0, 96), (1, 8)), -0.2, 0.2), 1.1953125, 2.5).astype(jnp.bfloat16),
        "link_rows": draw_link_rows(jax.random.fold_in(key_list[8], 71), 0),
        "link_signs": draw_link_signs(jax.random.fold_in(key_list[8], 71), 0),
        "link_counts": draw_link_counts(jax.random.fold_in(key_list[8], 71), 0),
    }


def build_block(packed, diag, flex):
    size = packed.shape[0]
    row_ids = lax.broadcasted_iota(jnp.int32, (size, size), 0)
    col_ids = lax.broadcasted_iota(jnp.int32, (size, size), 1)
    mirror = packed.T
    if flex:
        return jnp.where(col_ids >= row_ids, packed, mirror)
    lower = jnp.where(row_ids > col_ids, packed, mirror)
    return jnp.where(row_ids == col_ids, diag[:, None], lower)

def local_term(block, scale, sign_row, field):
    operand = (scale[:, None] * sign_row[:, None] * field).astype(jnp.bfloat16)
    product = jnp.dot(block.astype(jnp.float32), operand.astype(jnp.float32), preferred_element_type=jnp.float32)
    return (sign_row[:, None] * scale[:, None] * product).astype(jnp.bfloat16)

def all_terms(packed_blocks, diag, scale, sign_rows, field, flex):
    lead = packed_blocks.shape[:2]
    count = lead[0] * lead[1]

    def single(items):
        block = build_block(items[0], items[1], flex)
        return local_term(block, items[2], items[3], items[4])
    terms = lax.map(single, (packed_blocks.reshape((count,) + packed_blocks.shape[2:]), diag.reshape(count, -1), scale.reshape(count, -1), sign_rows.reshape(count, -1), field.reshape((count,) + field.shape[2:])))
    return terms.reshape(lead + terms.shape[1:])

def live_slots(link_counts, slots):
    return lax.broadcasted_iota(jnp.int32, link_counts.shape + (slots,), 3) < link_counts[..., None]

def assemble(term, link_rows, link_counts):
    spans, chords, four, slots = link_rows.shape
    width = term.shape[-1]
    flat_rows = link_rows.reshape(spans, chords, four * slots).astype(jnp.int32)
    sent = jnp.take_along_axis(term, flat_rows[..., None], axis=2).reshape(spans, chords, four, slots, width)
    valid = live_slots(link_counts, slots)[..., None]
    sent = jnp.where(valid, sent, jnp.zeros_like(sent))
    zero_span = jnp.zeros_like(sent[:1, :, 0])
    zero_chord = jnp.zeros_like(sent[:, :1, 0])
    from_lower_span = jnp.concatenate([zero_span, sent[:-1, :, 1]], axis=0)
    from_upper_span = jnp.concatenate([sent[1:, :, 0], zero_span], axis=0)
    from_lower_chord = jnp.concatenate([zero_chord, sent[:, :-1, 3]], axis=1)
    from_upper_chord = jnp.concatenate([sent[:, 1:, 2], zero_chord], axis=1)
    received = jnp.stack([from_lower_span, from_upper_span, from_lower_chord, from_upper_chord], axis=2)
    received = jnp.where(valid, received, jnp.zeros_like(received))
    total = (sent.astype(jnp.float32) + received.astype(jnp.float32)).reshape(spans, chords, four * slots, width)

    def place(rows, values):
        return jnp.zeros((term.shape[2], width), jnp.float32).at[rows].set(values)
    return jax.vmap(jax.vmap(place))(flat_rows, total)

def make_sign_rows(link_rows, link_signs, link_counts, rows_total):
    spans, chords, four, slots = link_rows.shape
    valid = live_slots(link_counts, slots)
    values = jnp.where(valid, link_signs, 0).astype(jnp.float32).reshape(spans, chords, four * slots)
    flat_rows = link_rows.reshape(spans, chords, four * slots).astype(jnp.int32)

    def place(rows, vals):
        return jnp.zeros((rows_total,), jnp.float32).at[rows].set(vals)
    return jax.vmap(jax.vmap(place))(flat_rows, values)

def gram(left, right):
    return 0.5 * jnp.einsum('scrk,scrl->kl', left, right, precision=lax.Precision.HIGHEST)

def spd_solve(matrix, rhs):
    factor = jnp.linalg.cholesky(matrix)
    return jax.scipy.linalg.cho_solve((factor, True), rhs)

def mat_right(field, small):
    return jnp.einsum('scrk,kl->scrl', field, small, precision=lax.Precision.HIGHEST)

def reference(displacement, packed_blocks, flex_scale, dirichlet_scale, dirichlet_diag, link_rows, link_signs, link_counts):
    sign_rows = make_sign_rows(link_rows, link_signs, link_counts, packed_blocks.shape[2])

    def flex_apply(field):
        return assemble(all_terms(packed_blocks, dirichlet_diag, flex_scale, sign_rows, field, True), link_rows, link_counts)

    def dirichlet_apply(field):
        return assemble(all_terms(packed_blocks, dirichlet_diag, dirichlet_scale, sign_rows, field, False), link_rows, link_counts)
    gap_term = (sign_rows[..., None] * displacement.astype(jnp.float32)).astype(jnp.bfloat16)
    right = assemble(gap_term, link_rows, link_counts)
    multipliers = jnp.zeros_like(right)
    residual = right
    precond = dirichlet_apply(residual)
    direction = precond
    gamma = gram(precond, residual)
    for step in range(ITERS):
        image = flex_apply(direction)
        curv = gram(direction, image)
        alpha = spd_solve(curv, gamma)
        multipliers = multipliers + mat_right(direction, alpha)
        residual = residual - mat_right(image, alpha)
        if step + 1 < ITERS:
            precond = dirichlet_apply(residual)
            gamma_new = gram(precond, residual)
            beta = spd_solve(gamma, gamma_new)
            direction = precond + mat_right(direction, beta)
            gamma = gamma_new
    return (multipliers, residual)
```

```python
import functools

import jax
import jax.numpy as jnp
from jax import lax
from jax.experimental import pallas as pl
from jax.experimental.pallas import tpu as pltpu
from jax.sharding import Mesh, PartitionSpec as P

X_CHIPS, CORES = 4, 2
SPAN = ("z", "x", "core")
PLANE = ("x", "core", "y")

BF, F32 = jnp.bfloat16, jnp.float32
TILE = 256
VM = pl.BlockSpec(memory_space=pltpu.VMEM)
SM = pl.BlockSpec(memory_space=pltpu.SMEM)


def call(body, outs, in_specs, scratch=(), flops=10**8, moved=4 * 10**6):
    return pl.pallas_call(
        body,
        out_shape=[jax.ShapeDtypeStruct(shape, dtype) for shape, dtype in outs],
        in_specs=in_specs,
        out_specs=[VM] * len(outs),
        scratch_shapes=list(scratch),
        compiler_params=pltpu.CompilerParams(vmem_limit_bytes=16 * 2**20),
        cost_estimate=pl.CostEstimate(flops=flops, bytes_accessed=moved, transcendentals=0),
    )


def mm(a, b):
    return jnp.dot(a, b, preferred_element_type=F32)


def gram_of(a, b):
    return lax.dot_general(a, b, (((0,), (0,)), ((), ())), preferred_element_type=F32)


def columns(pieces):
    return jnp.concatenate([p.astype(F32) for p in pieces], axis=0).T


def pack_kernel(rows, signs, counts, disp, pick, sent):
    slots = rows.shape[3]
    per = slots // 128
    parts = [(d, h) for d in range(4) for h in range(per)]
    row_cols = columns([rows[0, 0, d : d + 1, h * 128 : (h + 1) * 128] for d, h in parts])
    sign_cols = columns([signs[0, 0, d : d + 1, h * 128 : (h + 1) * 128] for d, h in parts])
    row_cols = row_cols.astype(jnp.int32)
    lanes = lax.broadcasted_iota(jnp.int32, (128, pick.shape[1]), 1)
    place = lax.broadcasted_iota(jnp.int32, (128, 1), 0)
    for j, (d, h) in enumerate(parts):
        here = slice(j * 128, (j + 1) * 128)
        pick[here, :] = jnp.where(lanes == row_cols[:, j : j + 1], 1.0, 0.0).astype(BF)
        live = place + h * 128 < counts[0, 0, d]
        sign = jnp.where(live, sign_cols[:, j : j + 1], 0.0)
        sent[here, :] = (sign * mm(pick[here, :], disp[...])).astype(BF)


def build_kernel(rows, signs, counts, disp, packed, diag, put, sign_row, gap, flex, diri, live_sign):
    slots = rows.shape[3]
    size = put.shape[0]
    per = slots // 128
    parts = [(d, h) for d in range(4) for h in range(per)]
    sign_cols = columns([signs[0, 0, d : d + 1, h * 128 : (h + 1) * 128] for d, h in parts])
    place = lax.broadcasted_iota(jnp.int32, (128, 1), 0)
    for j, (d, h) in enumerate(parts):
        live = place + h * 128 < counts[0, 0, d]
        sign = jnp.where(live, sign_cols[:, j : j + 1], 0.0)
        live_sign[j * 128 : (j + 1) * 128, :] = jnp.broadcast_to(sign, (128, 128)).astype(BF)
    down = lax.broadcasted_iota(jnp.int32, (128, slots), 0)
    for i in range(size // 128):
        here = slice(i * 128, (i + 1) * 128)
        for d in range(4):
            hit = down + i * 128 == rows[0, 0, d : d + 1, :]
            put[here, d * slots : (d + 1) * slots] = jnp.where(hit, 1.0, 0.0).astype(BF)
        sign = mm(put[here, :], live_sign[...])
        sign_row[here, :] = sign.astype(BF)
        gap[here, :] = (sign * disp[here, :].astype(F32)).astype(BF)
    r = lax.broadcasted_iota(jnp.int32, (128, 128), 0)
    c = lax.broadcasted_iota(jnp.int32, (128, 128), 1)
    for i in range(size // 128):
        a = slice(i * 128, (i + 1) * 128)
        for j in range(i + 1, size // 128):
            b = slice(j * 128, (j + 1) * 128)
            upper, lower = packed[a, b], packed[b, a]
            flex[a, b] = upper
            flex[b, a] = upper.T
            diri[b, a] = lower
            diri[a, b] = lower.T
        own = packed[a, a].astype(F32)
        turned = own.T
        flex[a, a] = jnp.where(c >= r, own, turned).astype(BF)
        low = jnp.where(r > c, own, turned)
        diri[a, a] = jnp.where(r == c, diag[0, :, a].astype(F32), low).astype(BF)


def apply_kernel(put, pick, block, sign_row, scale, base, r0, r1, r2, r3, partner, term, sent, operand):
    size = put.shape[0]
    scale_cols = columns([scale[0, :, i * 128 : (i + 1) * 128] for i in range(size // 128)])
    factors = []
    for i in range(size // TILE):
        here = slice(i * TILE, (i + 1) * TILE)
        got = None
        for d, r in enumerate((r0, r1, r2, r3)):
            slots = r.shape[0]
            piece = mm(put[here, d * slots : (d + 1) * slots], r[...])
            got = piece if got is None else got + piece
        partner[here, :] = got.astype(BF)
        each = TILE // 128
        column = jnp.concatenate([scale_cols[:, i * each + k : i * each + k + 1] for k in range(each)], axis=0)
        factor = column * sign_row[here, :].astype(F32)
        operand[here, :] = (factor * (base[here, :].astype(F32) + got)).astype(BF)
    for i in range(size // TILE):
        here = slice(i * TILE, (i + 1) * TILE)
        each = TILE // 128
        column = jnp.concatenate([scale_cols[:, i * each + k : i * each + k + 1] for k in range(each)], axis=0)
        factor = column * sign_row[here, :].astype(F32)
        term[here, :] = (factor * mm(block[here, :], operand[...])).astype(BF)
    for i in range(size // TILE):
        here = slice(i * TILE, (i + 1) * TILE)
        sent[here, :] = mm(pick[here, :], term[...]).astype(BF)


def gram_kernel(base, partner, term, out):
    out[...] = gram_of(base[...], term[...]) + gram_of(partner[...], term[...])


def split3(value):
    high = value.astype(BF)
    rest = value - high.astype(F32)
    mid = rest.astype(BF)
    return high, mid, (rest - mid.astype(F32)).astype(BF)


def finish_kernel(put, r0, r1, r2, r3, gap, part0, term1, part1, term2, alpha, mult, resid):
    size = put.shape[0]
    pieces = split3(alpha[...])
    for i in range(size // TILE):
        here = slice(i * TILE, (i + 1) * TILE)
        got = None
        for d, r in enumerate((r0, r1, r2, r3)):
            slots = r.shape[0]
            piece = mm(put[here, d * slots : (d + 1) * slots], r[...])
            got = piece if got is None else got + piece
        got = got.astype(BF)
        step = sum(mm(f, p) for p in pieces[::-1] for f in (term1[here, :], part1[here, :]))
        mult[here, :] = step
        step = sum(mm(f, p) for p in pieces[::-1] for f in (term2[here, :], got))
        resid[here, :] = gap[here, :].astype(F32) + part0[here, :].astype(F32) - step


def exchange(sent, slots, sizes):
    span_count, chord_count = sizes
    up = lambda n: [(i, i + 1) for i in range(n - 1)]
    down = lambda n: [(i + 1, i) for i in range(n - 1)]
    piece = [sent[d * slots : (d + 1) * slots] for d in range(4)]
    return (
        lax.ppermute(piece[1], SPAN, up(span_count)),
        lax.ppermute(piece[0], SPAN, down(span_count)),
        lax.ppermute(piece[3], "y", up(chord_count)),
        lax.ppermute(piece[2], "y", down(chord_count)),
    )


def reduce_all(value):
    rows, width = value.shape
    plane = lax.axis_size(PLANE)
    height = lax.axis_size("z")
    chunks = lax.all_to_all(value.reshape(plane, rows // plane, width), PLANE, 0, 0)
    chunk = jnp.sum(chunks, axis=0)
    layers = lax.all_to_all(jnp.broadcast_to(chunk[None], (height,) + chunk.shape), "z", 0, 0)
    chunk = jnp.sum(layers, axis=0)
    whole = lax.all_to_all(jnp.broadcast_to(chunk[None], (plane,) + chunk.shape), PLANE, 0, 0)
    return whole.reshape(rows, width)


def spd_solve(matrix, rhs):
    factor = jnp.linalg.cholesky(matrix)
    return jax.scipy.linalg.cho_solve((factor, True), rhs)


def shards(sizes, disp, packed, fscale, dscale, diag, rows, signs, counts):
    size, width = disp.shape[2:]
    slots = rows.shape[3]
    disp, packed = disp[0, 0], packed[0, 0]
    field = ((size, width), BF)
    square = ((size, size), BF)
    pick, sent = call(pack_kernel, [square, field], [VM, VM, SM, VM])(rows, signs, counts, disp)
    got0 = exchange(sent, slots, sizes)
    put, sign_row, gap, flex, diri = call(
        build_kernel,
        [square, field, field, square, square],
        [VM, VM, SM, VM, VM, VM],
        [pltpu.VMEM((size, width), BF)],
    )(rows, signs, counts, disp, packed, diag)

    def operate(block, scale, base, got):
        return call(apply_kernel, [field] * 3, [VM] * 10, [pltpu.VMEM((size, width), BF)], flops=8 * 10**8)(
            put, pick, block, sign_row, scale, base, *got
        )

    def local_gram(base, partner, term):
        return call(gram_kernel, [((width, width), F32)], [VM] * 3)(base, partner, term)[0]

    part0, term1, sent = operate(diri, dscale, gap, got0)
    got1 = exchange(sent, slots, sizes)
    gamma = local_gram(gap, part0, term1)
    part1, term2, sent = operate(flex, fscale, term1, got1)
    got2 = exchange(sent, slots, sizes)
    curv = local_gram(term1, part1, term2)
    both = reduce_all(jnp.concatenate([gamma, curv], axis=0))
    alpha = spd_solve(both[width:], both[:width])
    mult, resid = call(finish_kernel, [((size, width), F32)] * 2, [VM] * 11)(
        put, *got2, gap, part0, term1, part1, term2, alpha
    )
    return mult[None, None], resid[None, None]


def solution(mesh):
    span_count, chord_count = mesh.shape["span"], mesh.shape["chord"]
    grid = (span_count // (X_CHIPS * CORES), X_CHIPS, CORES, chord_count)
    fine = Mesh(mesh.devices.reshape(grid), SPAN + ("y",))
    spec = lambda extra: P(SPAN, "y", *([None] * extra))
    return jax.shard_map(
        functools.partial(shards, (span_count, chord_count)),
        mesh=fine,
        in_specs=tuple(spec(n) for n in (2, 2, 1, 1, 1, 2, 2, 1)),
        out_specs=(spec(2), spec(2)),
        check_vma=False,
    )
```

```python
import functools

import jax
import jax.numpy as jnp
from jax import lax
from jax.experimental import pallas as pl
from jax.experimental.pallas import tpu as pltpu
from jax.sharding import Mesh, PartitionSpec as P

X_CHIPS, CORES = 4, 2
SPAN = ("z", "x", "core")
PLANE = ("x", "core", "y")

BF, F32 = jnp.bfloat16, jnp.float32
TILE = 256
STEP = 4
VM = pl.BlockSpec(memory_space=pltpu.VMEM)
HB = pl.BlockSpec(memory_space=pltpu.HBM)


def call(body, outs, in_specs, scratch=(), flops=10**8, moved=4 * 10**6, out_spec=VM):
    return pl.pallas_call(
        body,
        out_shape=[jax.ShapeDtypeStruct(shape, dtype) for shape, dtype in outs],
        in_specs=in_specs,
        out_specs=[out_spec] * len(outs),
        scratch_shapes=list(scratch),
        compiler_params=pltpu.CompilerParams(vmem_limit_bytes=16 * 2**20),
        cost_estimate=pl.CostEstimate(flops=flops, bytes_accessed=moved, transcendentals=0),
    )


def mm(a, b):
    return jnp.dot(a, b, preferred_element_type=F32)


def gram_of(a, b):
    return lax.dot_general(a, b, (((0,), (0,)), ((), ())), preferred_element_type=F32)


def columns(pieces):
    return jnp.concatenate([p.astype(F32) for p in pieces], axis=0).T


def pack_kernel(
    rows, signs, counts, disp, packed, diag, dscale, fscale,
    pick, s0, s1, s2, s3, live_sign, rows_v, disp_v, packed_v, diag_v, dscale_v, fscale_v,
    signs_v, counts_s, sems,
):
    moves = [
        pltpu.make_async_copy(src, dst, sems.at[i])
        for i, (src, dst) in enumerate(
            (
                (rows, rows_v), (signs, signs_v), (counts, counts_s), (disp, disp_v),
                (packed, packed_v), (diag, diag_v), (dscale, dscale_v), (fscale, fscale_v),
            )
        )
    ]
    for move in moves:
        move.start()
    slots = rows_v.shape[3]
    per = slots // 128
    parts = [(d, h) for d in range(4) for h in range(per)]
    moves[0].wait()
    row_cols = columns([rows_v[0, 0, d : d + 1, h * 128 : (h + 1) * 128] for d, h in parts])
    row_cols = row_cols.astype(jnp.int32)
    moves[1].wait()
    sign_cols = columns([signs_v[0, 0, d : d + 1, h * 128 : (h + 1) * 128] for d, h in parts])
    moves[2].wait()
    moves[3].wait()
    lanes = lax.broadcasted_iota(jnp.int32, (128, pick.shape[1]), 1)
    place = lax.broadcasted_iota(jnp.int32, (128, 1), 0)
    for j, (d, h) in enumerate(parts):
        here = slice(j * 128, (j + 1) * 128)
        pick[here, :] = jnp.where(lanes == row_cols[:, j : j + 1], 1.0, 0.0).astype(BF)
        live = place + h * 128 < counts_s[0, 0, d]
        sign = jnp.where(live, sign_cols[:, j : j + 1], 0.0)
        live_sign[here, :] = jnp.broadcast_to(sign, (128, 128)).astype(BF)
        sent = (s0, s1, s2, s3)[d]
        sent[h * 128 : (h + 1) * 128, :] = (sign * mm(pick[here, :], disp_v[...])).astype(BF)
    for move in moves[4:]:
        move.wait()


def build_kernel(rows, live_sign, disp, packed, diag, put, sign_row, gap, flex, diri):
    slots = rows.shape[3]
    size = put.shape[0]
    down = lax.broadcasted_iota(jnp.int32, (128, slots), 0)
    for i in range(size // 128):
        here = slice(i * 128, (i + 1) * 128)
        for d in range(4):
            hit = down + i * 128 == rows[0, 0, d : d + 1, :]
            put[here, d * slots : (d + 1) * slots] = jnp.where(hit, 1.0, 0.0).astype(BF)
        sign = mm(put[here, :], live_sign[...])
        sign_row[here, :] = sign.astype(BF)
        gap[here, :] = (sign * disp[here, :].astype(F32)).astype(BF)
    r = lax.broadcasted_iota(jnp.int32, (128, 128), 0)
    c = lax.broadcasted_iota(jnp.int32, (128, 128), 1)
    for i in range(size // 128):
        a = slice(i * 128, (i + 1) * 128)
        for j in range(i + 1, size // 128):
            b = slice(j * 128, (j + 1) * 128)
            upper, lower = packed[a, b], packed[b, a]
            flex[a, b] = upper
            flex[b, a] = upper.T
            diri[b, a] = lower
            diri[a, b] = lower.T
        own = packed[a, a].astype(F32)
        turned = own.T
        flex[a, a] = jnp.where(c >= r, own, turned).astype(BF)
        low = jnp.where(r > c, own, turned)
        diri[a, a] = jnp.where(r == c, diag[0, :, a].astype(F32), low).astype(BF)


def apply_kernel(put, pick, block, sign_row, scale, base, r0, r1, r2, r3, partner, term, s0, s1, s2, s3, operand):
    size = put.shape[0]
    scale_cols = columns([scale[0, :, i * 128 : (i + 1) * 128] for i in range(size // 128)])
    factors = []
    for i in range(size // TILE):
        here = slice(i * TILE, (i + 1) * TILE)
        got = None
        for d, r in enumerate((r0, r1, r2, r3)):
            slots = r.shape[0]
            piece = mm(put[here, d * slots : (d + 1) * slots], r[...])
            got = piece if got is None else got + piece
        partner[here, :] = got.astype(BF)
        each = TILE // 128
        column = jnp.concatenate([scale_cols[:, i * each + k : i * each + k + 1] for k in range(each)], axis=0)
        factor = column * sign_row[here, :].astype(F32)
        operand[here, :] = (factor * (base[here, :].astype(F32) + got)).astype(BF)
    for i in range(size // TILE):
        here = slice(i * TILE, (i + 1) * TILE)
        each = TILE // 128
        column = jnp.concatenate([scale_cols[:, i * each + k : i * each + k + 1] for k in range(each)], axis=0)
        factor = column * sign_row[here, :].astype(F32)
        term[here, :] = (factor * mm(block[here, :], operand[...])).astype(BF)
    for d, sent in enumerate((s0, s1, s2, s3)):
        slots = sent.shape[0]
        sent[...] = mm(pick[d * slots : (d + 1) * slots, :], term[...]).astype(BF)


def gram_kernel(base, partner, term, out):
    out[...] = gram_of(base[...], term[...]) + gram_of(partner[...], term[...])


def split3(value):
    high = value.astype(BF)
    rest = value - high.astype(F32)
    mid = rest.astype(BF)
    return high, mid, (rest - mid.astype(F32)).astype(BF)


def small_solve(p, r):
    n = len(p)
    if n == 2:
        scale = 1.0 / (p[0][0] * p[1][1] - p[0][1] * p[1][0])
        return [
            (p[1][1] * scale) * r[0] - (p[0][1] * scale) * r[1],
            (p[0][0] * scale) * r[1] - (p[1][0] * scale) * r[0],
        ]
    h = n // 2
    one, rest = range(h), range(h, n)
    a = [row[:h] for row in p[:h]]
    across = [small_solve(a, [p[i][j] for i in one]) for j in rest]
    u = small_solve(a, r[:h])
    schur = [[p[i][h + j] - sum(p[i][k] * across[j][k] for k in one) for j in range(n - h)] for i in rest]
    v = small_solve(schur, [r[i] - sum(p[i][k] * u[k] for k in one) for i in rest])
    return [u[i] - sum(across[j][i] * v[j] for j in range(n - h)) for i in one] + v


def solve_kernel(both, alpha):
    width = alpha.shape[0]
    count = width // 8
    rows = both.shape[1]

    def tile(t):
        if rows >= 8:
            return both[t * 8 // rows, t * 8 % rows : t * 8 % rows + 8]
        return jnp.concatenate([both[t * (8 // rows) + k] for k in range(8 // rows)], axis=0)

    g = [tile(t) for t in range(count)]
    curv = jnp.concatenate([tile(count + t) for t in range(count)], axis=0)
    curv = (curv + curv.T) * 0.5
    a = [curv[8 * t : 8 * t + 8, :] for t in range(count)]
    spot = lax.broadcasted_iota(jnp.int32, (8, width), 0)
    for j in range(0, width, STEP):
        cols = [[jnp.broadcast_to(a[t][:, j + k : j + k + 1], (8, width)) for k in range(STEP)] for t in range(count)]
        own, r0 = j // 8, j % 8
        row = lambda x, k: jnp.broadcast_to(x[r0 + k : r0 + k + 1, :], (8, width))
        p = [[row(cols[own][l], k) for l in range(STEP)] for k in range(STEP)]
        na = small_solve(p, [row(a[own], k) for k in range(STEP)])
        ng = small_solve(p, [row(g[own], k) for k in range(STEP)])
        for t in range(count):
            ua = a[t] - sum(cols[t][k] * na[k] for k in range(STEP))
            ug = g[t] - sum(cols[t][k] * ng[k] for k in range(STEP))
            if t == own:
                for k in range(STEP):
                    ua = jnp.where(spot == r0 + k, na[k], ua)
                    ug = jnp.where(spot == r0 + k, ng[k], ug)
            a[t], g[t] = ua, ug
    for t in range(count):
        alpha[8 * t : 8 * t + 8, :] = g[t]


def finish_kernel(put, r0, r1, r2, r3, gap, part0, term1, part1, term2, alpha, mult, resid, mult_v, resid_v, sems):
    size = put.shape[0]
    pieces = split3(alpha[...])
    moves = []
    for i in range(size // TILE):
        here = slice(i * TILE, (i + 1) * TILE)
        mult_v[here, :] = sum(mm(f, p) for p in pieces[::-1] for f in (term1[here, :], part1[here, :]))
        moves.append(pltpu.make_async_copy(mult_v.at[here, :], mult.at[here, :], sems.at[0, i]))
        moves[-1].start()
        got = None
        for d, r in enumerate((r0, r1, r2, r3)):
            slots = r.shape[0]
            piece = mm(put[here, d * slots : (d + 1) * slots], r[...])
            got = piece if got is None else got + piece
        got = got.astype(BF)
        step = sum(mm(f, p) for p in pieces[::-1] for f in (term2[here, :], got))
        resid_v[here, :] = gap[here, :].astype(F32) + part0[here, :].astype(F32) - step
        moves.append(pltpu.make_async_copy(resid_v.at[here, :], resid.at[here, :], sems.at[1, i]))
        moves[-1].start()
    for move in moves:
        move.wait()


def exchange(piece, sizes):
    span_count, chord_count = sizes
    up = lambda n: [(i, i + 1) for i in range(n - 1)]
    down = lambda n: [(i + 1, i) for i in range(n - 1)]
    return (
        lax.ppermute(piece[1], SPAN, up(span_count)),
        lax.ppermute(piece[0], SPAN, down(span_count)),
        lax.ppermute(piece[3], "y", up(chord_count)),
        lax.ppermute(piece[2], "y", down(chord_count)),
    )


def reduce_all(value):
    rows, width = value.shape
    plane = lax.axis_size(PLANE)
    height = lax.axis_size("z")
    chunks = lax.all_to_all(value.reshape(plane, rows // plane, width), PLANE, 0, 0)
    chunk = jnp.sum(chunks, axis=0)
    layers = lax.all_to_all(jnp.broadcast_to(chunk[None], (height,) + chunk.shape), "z", 0, 0)
    chunk = jnp.sum(layers, axis=0)
    whole = lax.all_to_all(jnp.broadcast_to(chunk[None], (plane,) + chunk.shape), PLANE, 0, 0)
    return whole


def shards(sizes, disp, packed, fscale, dscale, diag, rows, signs, counts):
    size, width = disp.shape[2:]
    slots = rows.shape[3]
    disp, packed = disp[0, 0], packed[0, 0]
    field, square, piece = ((size, width), BF), ((size, size), BF), ((slots, width), BF)
    like = lambda x: (x.shape, x.dtype)
    pick, *out = call(
        pack_kernel,
        [square] + [piece] * 4 + [field] + [like(x) for x in (rows, disp, packed, diag, dscale, fscale)],
        [HB] * 8,
        [pltpu.VMEM(signs.shape, signs.dtype), pltpu.SMEM(counts.shape, counts.dtype), pltpu.SemaphoreType.DMA((8,))],
    )(*(pltpu.with_memory_space_constraint(x, pltpu.HBM) for x in (rows, signs, counts, disp, packed, diag, dscale, fscale)))
    live_sign, rows, disp, packed, diag, dscale, fscale = out[4:]
    got0 = exchange(out[:4], sizes)
    put, sign_row, gap, flex, diri = call(build_kernel, [square, field, field, square, square], [VM] * 5)(
        rows, live_sign, disp, packed, diag
    )

    def operate(block, scale, base, got):
        part, term, *sent = call(
            apply_kernel, [field] * 2 + [piece] * 4, [VM] * 10, [pltpu.VMEM((size, width), BF)], flops=8 * 10**8
        )(put, pick, block, sign_row, scale, base, *got)
        return part, term, sent

    def local_gram(base, partner, term):
        return call(gram_kernel, [((width, width), F32)], [VM] * 3)(base, partner, term)[0]

    part0, term1, sent = operate(diri, dscale, gap, got0)
    got1 = exchange(sent, sizes)
    gamma = local_gram(gap, part0, term1)
    part1, term2, sent = operate(flex, fscale, term1, got1)
    got2 = exchange(sent, sizes)
    curv = local_gram(term1, part1, term2)
    both = reduce_all(jnp.concatenate([gamma, curv], axis=0))
    alpha = call(solve_kernel, [((width, width), F32)], [VM])(both)[0]
    whole = ((size, width), F32)
    mult, resid = call(
        finish_kernel,
        [whole] * 2,
        [VM] * 11,
        [pltpu.VMEM(*whole), pltpu.VMEM(*whole), pltpu.SemaphoreType.DMA((2, size // TILE))],
        out_spec=HB,
    )(put, *got2, gap, part0, term1, part1, term2, alpha)
    return mult[None, None], resid[None, None]


def solution(mesh):
    span_count, chord_count = mesh.shape["span"], mesh.shape["chord"]
    grid = (span_count // (X_CHIPS * CORES), X_CHIPS, CORES, chord_count)
    fine = Mesh(mesh.devices.reshape(grid), SPAN + ("y",))
    spec = lambda extra: P(SPAN, "y", *([None] * extra))
    return jax.shard_map(
        functools.partial(shards, (span_count, chord_count)),
        mesh=fine,
        in_specs=tuple(spec(n) for n in (2, 2, 1, 1, 1, 2, 2, 1)),
        out_specs=(spec(2), spec(2)),
        check_vma=False,
    )
```

```python
import functools

import jax
import jax.numpy as jnp
from jax import lax
from jax.experimental import pallas as pl
from jax.experimental.pallas import tpu as pltpu
from jax.sharding import Mesh, PartitionSpec as P


X_CHIPS, CORES = 4, 2
SPAN = ("z", "x", "core")
PLANE = ("x", "core", "y")

BF, F32 = jnp.bfloat16, jnp.float32
TILE = 256
STEP = 4
VM = pl.BlockSpec(memory_space=pltpu.VMEM)
HB = pl.BlockSpec(memory_space=pltpu.HBM)


def call(body, outs, in_specs, scratch=(), flops=10**8, moved=4 * 10**6, out_spec=VM):
    return pl.pallas_call(
        body,
        out_shape=[jax.ShapeDtypeStruct(shape, dtype) for shape, dtype in outs],
        in_specs=in_specs,
        out_specs=[out_spec] * len(outs),
        scratch_shapes=list(scratch),
        compiler_params=pltpu.CompilerParams(vmem_limit_bytes=16 * 2**20),
        cost_estimate=pl.CostEstimate(flops=flops, bytes_accessed=moved, transcendentals=0),
    )


def mm(a, b):
    return jnp.dot(a, b, preferred_element_type=F32)


def gram_of(a, b):
    return lax.dot_general(a, b, (((0,), (0,)), ((), ())), preferred_element_type=F32)


def columns(pieces):
    return jnp.concatenate([p.astype(F32) for p in pieces], axis=0).T


def pack_kernel(
    rows, signs, counts, disp, packed, diag, dscale, fscale,
    pick, s0, s1, s2, s3, live_sign, rows_v, disp_v, packed_v, diag_v, dscale_v, fscale_v,
    signs_v, counts_s, sems,
):
    moves = [
        pltpu.make_async_copy(src, dst, sems.at[i])
        for i, (src, dst) in enumerate(
            (
                (rows, rows_v), (signs, signs_v), (counts, counts_s), (disp, disp_v),
                (packed, packed_v), (diag, diag_v), (dscale, dscale_v), (fscale, fscale_v),
            )
        )
    ]
    for move in moves:
        move.start()
    slots = rows_v.shape[3]
    per = slots // 128
    parts = [(d, h) for d in range(4) for h in range(per)]
    moves[0].wait()
    row_cols = columns([rows_v[0, 0, d : d + 1, h * 128 : (h + 1) * 128] for d, h in parts])
    row_cols = row_cols.astype(jnp.int32)
    moves[1].wait()
    sign_cols = columns([signs_v[0, 0, d : d + 1, h * 128 : (h + 1) * 128] for d, h in parts])
    moves[2].wait()
    moves[3].wait()
    lanes = lax.broadcasted_iota(jnp.int32, (128, pick.shape[1]), 1)
    place = lax.broadcasted_iota(jnp.int32, (128, 1), 0)
    for j, (d, h) in enumerate(parts):
        here = slice(j * 128, (j + 1) * 128)
        pick[here, :] = jnp.where(lanes == row_cols[:, j : j + 1], 1.0, 0.0).astype(BF)
        live = place + h * 128 < counts_s[0, 0, d]
        sign = jnp.where(live, sign_cols[:, j : j + 1], 0.0)
        live_sign[here, :] = jnp.broadcast_to(sign, (128, 128)).astype(BF)
        sent = (s0, s1, s2, s3)[d]
        sent[h * 128 : (h + 1) * 128, :] = (sign * mm(pick[here, :], disp_v[...])).astype(BF)
    for move in moves[4:]:
        move.wait()


def build_kernel(rows, live_sign, disp, packed, diag, put, sign_row, gap, flex, diri):
    slots = rows.shape[3]
    size = put.shape[0]
    down = lax.broadcasted_iota(jnp.int32, (128, slots), 0)
    for i in range(size // 128):
        here = slice(i * 128, (i + 1) * 128)
        for d in range(4):
            hit = down + i * 128 == rows[0, 0, d : d + 1, :]
            put[here, d * slots : (d + 1) * slots] = jnp.where(hit, 1.0, 0.0).astype(BF)
        sign = mm(put[here, :], live_sign[...])
        sign_row[here, :] = sign.astype(BF)
        gap[here, :] = (sign * disp[here, :].astype(F32)).astype(BF)
    r = lax.broadcasted_iota(jnp.int32, (128, 128), 0)
    c = lax.broadcasted_iota(jnp.int32, (128, 128), 1)
    for i in range(size // 128):
        a = slice(i * 128, (i + 1) * 128)
        for j in range(i + 1, size // 128):
            b = slice(j * 128, (j + 1) * 128)
            upper, lower = packed[a, b], packed[b, a]
            flex[a, b] = upper
            flex[b, a] = upper.T
            diri[b, a] = lower
            diri[a, b] = lower.T
        own = packed[a, a].astype(F32)
        turned = own.T
        flex[a, a] = jnp.where(c >= r, own, turned).astype(BF)
        low = jnp.where(r > c, own, turned)
        diri[a, a] = jnp.where(r == c, diag[0, :, a].astype(F32), low).astype(BF)


def apply_kernel(put, pick, block, sign_row, scale, base, r0, r1, r2, r3, partner, term, s0, s1, s2, s3, operand):
    size = put.shape[0]
    scale_cols = columns([scale[0, :, i * 128 : (i + 1) * 128] for i in range(size // 128)])
    for i in range(size // TILE):
        here = slice(i * TILE, (i + 1) * TILE)
        got = None
        for d, r in enumerate((r0, r1, r2, r3)):
            slots = r.shape[0]
            piece = mm(put[here, d * slots : (d + 1) * slots], r[...])
            got = piece if got is None else got + piece
        partner[here, :] = got.astype(BF)
        each = TILE // 128
        column = jnp.concatenate([scale_cols[:, i * each + k : i * each + k + 1] for k in range(each)], axis=0)
        factor = column * sign_row[here, :].astype(F32)
        operand[here, :] = (factor * (base[here, :].astype(F32) + got)).astype(BF)
    for i in range(size // TILE):
        here = slice(i * TILE, (i + 1) * TILE)
        each = TILE // 128
        column = jnp.concatenate([scale_cols[:, i * each + k : i * each + k + 1] for k in range(each)], axis=0)
        factor = column * sign_row[here, :].astype(F32)
        term[here, :] = (factor * mm(block[here, :], operand[...])).astype(BF)
    for d, sent in enumerate((s0, s1, s2, s3)):
        slots = sent.shape[0]
        sent[...] = mm(pick[d * slots : (d + 1) * slots, :], term[...]).astype(BF)


def gram_kernel(base, partner, term, out):
    out[...] = gram_of(base[...], term[...]) + gram_of(partner[...], term[...])


def split3(value):
    high = value.astype(BF)
    rest = value - high.astype(F32)
    mid = rest.astype(BF)
    return high, mid, (rest - mid.astype(F32)).astype(BF)


def small_solve(p, r):
    n = len(p)
    if n == 2:
        scale = 1.0 / (p[0][0] * p[1][1] - p[0][1] * p[1][0])
        return [
            (p[1][1] * scale) * r[0] - (p[0][1] * scale) * r[1],
            (p[0][0] * scale) * r[1] - (p[1][0] * scale) * r[0],
        ]
    h = n // 2
    one, rest = range(h), range(h, n)
    a = [row[:h] for row in p[:h]]
    across = [small_solve(a, [p[i][j] for i in one]) for j in rest]
    u = small_solve(a, r[:h])
    schur = [[p[i][h + j] - sum(p[i][k] * across[j][k] for k in one) for j in range(n - h)] for i in rest]
    v = small_solve(schur, [r[i] - sum(p[i][k] * u[k] for k in one) for i in rest])
    return [u[i] - sum(across[j][i] * v[j] for j in range(n - h)) for i in one] + v


def solve_kernel(both, alpha):
    width = alpha.shape[0]
    count = width // 8
    rows = both.shape[1]

    def tile(t):
        if rows >= 8:
            return both[t * 8 // rows, t * 8 % rows : t * 8 % rows + 8]
        return jnp.concatenate([both[t * (8 // rows) + k] for k in range(8 // rows)], axis=0)

    g = [tile(t) for t in range(count)]
    curv = jnp.concatenate([tile(count + t) for t in range(count)], axis=0)
    curv = (curv + curv.T) * 0.5
    a = [curv[8 * t : 8 * t + 8, :] for t in range(count)]
    spot = lax.broadcasted_iota(jnp.int32, (8, width), 0)
    for j in range(0, width, STEP):
        cols = [[jnp.broadcast_to(a[t][:, j + k : j + k + 1], (8, width)) for k in range(STEP)] for t in range(count)]
        own, r0 = j // 8, j % 8
        row = lambda x, k: jnp.broadcast_to(x[r0 + k : r0 + k + 1, :], (8, width))
        p = [[row(cols[own][l], k) for l in range(STEP)] for k in range(STEP)]
        na = small_solve(p, [row(a[own], k) for k in range(STEP)])
        ng = small_solve(p, [row(g[own], k) for k in range(STEP)])
        for t in range(count):
            ua = a[t] - sum(cols[t][k] * na[k] for k in range(STEP))
            ug = g[t] - sum(cols[t][k] * ng[k] for k in range(STEP))
            if t == own:
                for k in range(STEP):
                    ua = jnp.where(spot == r0 + k, na[k], ua)
                    ug = jnp.where(spot == r0 + k, ng[k], ug)
            a[t], g[t] = ua, ug
    for t in range(count):
        alpha[8 * t : 8 * t + 8, :] = g[t]


def place_kernel(first, rows, r0, r1, out):
    slots = r0.shape[0]
    down = lax.broadcasted_iota(jnp.int32, (TILE, slots), 0)
    for i in range(out.shape[0] // TILE):
        got = None
        for d, r in ((first, r0), (first + 1, r1)):
            hit = down + i * TILE == rows[0, 0, d : d + 1, :]
            piece = mm(jnp.where(hit, 1.0, 0.0).astype(BF), r[...])
            got = piece if got is None else got + piece
        out[i * TILE : (i + 1) * TILE, :] = got.astype(BF)


def finish_kernel(gap, part0, term1, part1, term2, span2, chord2, alpha, mult, resid, mult_v, resid_v, sems):
    size = gap.shape[0]
    pieces = split3(alpha[...])
    moves = []
    for i in range(size // TILE):
        here = slice(i * TILE, (i + 1) * TILE)
        mult_v[here, :] = sum(mm(f, p) for p in pieces[::-1] for f in (term1[here, :], part1[here, :]))
        moves.append(pltpu.make_async_copy(mult_v.at[here, :], mult.at[here, :], sems.at[0, i]))
        moves[-1].start()
        got = span2[here, :] + chord2[here, :]
        step = sum(mm(f, p) for p in pieces[::-1] for f in (term2[here, :], got))
        resid_v[here, :] = gap[here, :].astype(F32) + part0[here, :].astype(F32) - step
        moves.append(pltpu.make_async_copy(resid_v.at[here, :], resid.at[here, :], sems.at[1, i]))
        moves[-1].start()
    for move in moves:
        move.wait()


def exchange(piece, sizes):
    span_count, chord_count = sizes
    up = lambda n: [(i, i + 1) for i in range(n - 1)]
    down = lambda n: [(i + 1, i) for i in range(n - 1)]
    a = lax.ppermute(piece[1], SPAN, up(span_count))
    b = lax.ppermute(piece[0], SPAN, down(span_count))
    c = lax.ppermute(piece[3], "y", up(chord_count))
    d = lax.ppermute(piece[2], "y", down(chord_count))
    return a, b, c, d


def reduce_all(value):
    rows, width = value.shape
    plane = lax.axis_size(PLANE)
    height = lax.axis_size("z")
    chunks = lax.all_to_all(value.reshape(plane, rows // plane, width), PLANE, 0, 0)
    chunk = jnp.sum(chunks, axis=0)
    layers = lax.all_to_all(jnp.broadcast_to(chunk[None], (height,) + chunk.shape), "z", 0, 0)
    chunk = jnp.sum(layers, axis=0)
    return lax.all_to_all(jnp.broadcast_to(chunk[None], (plane,) + chunk.shape), PLANE, 0, 0)


def shards(sizes, disp, packed, fscale, dscale, diag, rows, signs, counts):
    size, width = disp.shape[2:]
    slots = rows.shape[3]
    disp, packed = disp[0, 0], packed[0, 0]
    field, square, piece = ((size, width), BF), ((size, size), BF), ((slots, width), BF)
    like = lambda x: (x.shape, x.dtype)
    pick, *out = call(
        pack_kernel,
        [square] + [piece] * 4 + [field] + [like(x) for x in (rows, disp, packed, diag, dscale, fscale)],
        [HB] * 8,
        [pltpu.VMEM(signs.shape, signs.dtype), pltpu.SMEM(counts.shape, counts.dtype), pltpu.SemaphoreType.DMA((8,))],
    )(*(pltpu.with_memory_space_constraint(x, pltpu.HBM) for x in (rows, signs, counts, disp, packed, diag, dscale, fscale)))
    live_sign, rows, disp, packed, diag, dscale, fscale = out[4:]
    got0 = exchange(out[:4], sizes)
    put, sign_row, gap, flex, diri = call(build_kernel, [square, field, field, square, square], [VM] * 5)(
        rows, live_sign, disp, packed, diag
    )

    def operate(block, scale, base, got):
        part, term, *sent = call(
            apply_kernel, [field] * 2 + [piece] * 4, [VM] * 10, [pltpu.VMEM((size, width), BF)], flops=8 * 10**8
        )(put, pick, block, sign_row, scale, base, *got)
        return part, term, sent

    def local_gram(base, partner, term):
        return call(gram_kernel, [((width, width), F32)], [VM] * 3)(base, partner, term)[0]

    part0, term1, sent = operate(diri, dscale, gap, got0)
    got1 = exchange(sent, sizes)
    gamma = local_gram(gap, part0, term1)
    part1, term2, sent = operate(flex, fscale, term1, got1)
    got2 = exchange(sent, sizes)
    curv = local_gram(term1, part1, term2)
    span2 = call(functools.partial(place_kernel, 0), [field], [VM] * 3)(rows, *got2[:2])[0]
    chord2 = call(functools.partial(place_kernel, 2), [field], [VM] * 3)(rows, *got2[2:])[0]
    both = reduce_all(jnp.concatenate([gamma, curv], axis=0))
    alpha = call(solve_kernel, [((width, width), F32)], [VM])(both)[0]
    whole = ((size, width), F32)
    mult, resid = call(
        finish_kernel,
        [whole] * 2,
        [VM] * 8,
        [pltpu.VMEM(*whole), pltpu.VMEM(*whole), pltpu.SemaphoreType.DMA((2, size // TILE))],
        out_spec=HB,
    )(gap, part0, term1, part1, term2, span2, chord2, alpha)
    return mult[None, None], resid[None, None]


def solution(mesh):
    span_count, chord_count = mesh.shape["span"], mesh.shape["chord"]
    grid = (span_count // (X_CHIPS * CORES), X_CHIPS, CORES, chord_count)
    fine = Mesh(mesh.devices.reshape(grid), SPAN + ("y",))
    spec = lambda extra: P(SPAN, "y", *([None] * extra))
    return jax.shard_map(
        functools.partial(shards, (span_count, chord_count)),
        mesh=fine,
        in_specs=tuple(spec(n) for n in (2, 2, 1, 1, 1, 2, 2, 1)),
        out_specs=(spec(2), spec(2)),
        check_vma=False,
    )
```

```python
import functools
import operator

import jax
import jax.numpy as jnp
from jax import lax
from jax.experimental import pallas as pl
from jax.experimental.pallas import tpu as pltpu
from jax.sharding import Mesh, PartitionSpec as P

X_CHIPS, CORES = 4, 2
SPAN = ("z", "x", "core")
PLANE = ("x", "core", "y")

BF, F32 = jnp.bfloat16, jnp.float32
TILE = 256
STEP, GROUP = 4, 8
VM = pl.BlockSpec(memory_space=pltpu.VMEM)
HB = pl.BlockSpec(memory_space=pltpu.HBM)


def call(body, outs, in_specs, scratch=(), flops=10**8, moved=4 * 10**6, out_spec=VM):
    return pl.pallas_call(
        body,
        out_shape=[jax.ShapeDtypeStruct(shape, dtype) for shape, dtype in outs],
        in_specs=in_specs,
        out_specs=[out_spec] * len(outs),
        scratch_shapes=list(scratch),
        compiler_params=pltpu.CompilerParams(vmem_limit_bytes=16 * 2**20),
        cost_estimate=pl.CostEstimate(flops=flops, bytes_accessed=moved, transcendentals=0),
    )


def mm(a, b):
    return jnp.dot(a, b, preferred_element_type=F32)


def gram_of(a, b):
    return lax.dot_general(a, b, (((0,), (0,)), ((), ())), preferred_element_type=F32)


def columns(pieces):
    return jnp.concatenate([p.astype(F32) for p in pieces], axis=0).T


def pack_kernel(
    rows, signs, counts, disp, packed, diag, dscale, fscale,
    pick, s0, s1, s2, s3, live_sign, rows_v, disp_v, packed_v, diag_v, dscale_v, fscale_v,
    signs_v, counts_s, sems,
):
    moves = [
        pltpu.make_async_copy(src, dst, sems.at[i])
        for i, (src, dst) in enumerate(
            (
                (rows, rows_v), (signs, signs_v), (counts, counts_s), (disp, disp_v),
                (packed, packed_v), (diag, diag_v), (dscale, dscale_v), (fscale, fscale_v),
            )
        )
    ]
    for move in moves:
        move.start()
    slots = rows_v.shape[3]
    per = slots // 128
    parts = [(d, h) for d in range(4) for h in range(per)]
    moves[0].wait()
    row_cols = columns([rows_v[0, 0, d : d + 1, h * 128 : (h + 1) * 128] for d, h in parts])
    row_cols = row_cols.astype(jnp.int32)
    moves[1].wait()
    sign_cols = columns([signs_v[0, 0, d : d + 1, h * 128 : (h + 1) * 128] for d, h in parts])
    moves[2].wait()
    moves[3].wait()
    lanes = lax.broadcasted_iota(jnp.int32, (128, pick.shape[1]), 1)
    place = lax.broadcasted_iota(jnp.int32, (128, 1), 0)
    for j, (d, h) in enumerate(parts):
        here = slice(j * 128, (j + 1) * 128)
        pick[here, :] = jnp.where(lanes == row_cols[:, j : j + 1], 1.0, 0.0).astype(BF)
        live = place + h * 128 < counts_s[0, 0, d]
        sign = jnp.where(live, sign_cols[:, j : j + 1], 0.0)
        live_sign[here, :] = jnp.broadcast_to(sign, (128, 128)).astype(BF)
        sent = (s0, s1, s2, s3)[d]
        sent[h * 128 : (h + 1) * 128, :] = (sign * mm(pick[here, :], disp_v[...])).astype(BF)
    for move in moves[4:]:
        move.wait()


def build_kernel(rows, live_sign, disp, packed, diag, put, sign_row, gap, flex, diri):
    slots = rows.shape[3]
    size = put.shape[0]
    down = lax.broadcasted_iota(jnp.int32, (128, slots), 0)
    for i in range(size // 128):
        here = slice(i * 128, (i + 1) * 128)
        for d in range(4):
            hit = down + i * 128 == rows[0, 0, d : d + 1, :]
            put[here, d * slots : (d + 1) * slots] = jnp.where(hit, 1.0, 0.0).astype(BF)
        sign = mm(put[here, :], live_sign[...])
        sign_row[here, :] = sign.astype(BF)
        gap[here, :] = (sign * disp[here, :].astype(F32)).astype(BF)
    r = lax.broadcasted_iota(jnp.int32, (128, 128), 0)
    c = lax.broadcasted_iota(jnp.int32, (128, 128), 1)
    for i in range(size // 128):
        a = slice(i * 128, (i + 1) * 128)
        for j in range(i + 1, size // 128):
            b = slice(j * 128, (j + 1) * 128)
            upper, lower = packed[a, b], packed[b, a]
            flex[a, b] = upper
            flex[b, a] = upper.T
            diri[b, a] = lower
            diri[a, b] = lower.T
        own = packed[a, a].astype(F32)
        turned = own.T
        flex[a, a] = jnp.where(c >= r, own, turned).astype(BF)
        low = jnp.where(r > c, own, turned)
        diri[a, a] = jnp.where(r == c, diag[0, :, a].astype(F32), low).astype(BF)


def apply_kernel(put, pick, block, sign_row, scale, base, r0, r1, r2, r3, partner, term, s0, s1, s2, s3, operand):
    size = put.shape[0]
    scale_cols = columns([scale[0, :, i * 128 : (i + 1) * 128] for i in range(size // 128)])
    factors = []
    for i in range(size // TILE):
        here = slice(i * TILE, (i + 1) * TILE)
        got = None
        for d, r in enumerate((r0, r1, r2, r3)):
            slots = r.shape[0]
            piece = mm(put[here, d * slots : (d + 1) * slots], r[...])
            got = piece if got is None else got + piece
        partner[here, :] = got.astype(BF)
        each = TILE // 128
        column = jnp.concatenate([scale_cols[:, i * each + k : i * each + k + 1] for k in range(each)], axis=0)
        factor = column * sign_row[here, :].astype(F32)
        operand[here, :] = (factor * (base[here, :].astype(F32) + got)).astype(BF)
    for i in range(size // TILE):
        here = slice(i * TILE, (i + 1) * TILE)
        each = TILE // 128
        column = jnp.concatenate([scale_cols[:, i * each + k : i * each + k + 1] for k in range(each)], axis=0)
        factor = column * sign_row[here, :].astype(F32)
        term[here, :] = (factor * mm(block[here, :], operand[...])).astype(BF)
    for d, sent in enumerate((s0, s1, s2, s3)):
        slots = sent.shape[0]
        sent[...] = mm(pick[d * slots : (d + 1) * slots, :], term[...]).astype(BF)


def gram_kernel(base, partner, term, out):
    out[...] = gram_of(base[...], term[...]) + gram_of(partner[...], term[...])


def split3(value):
    high = value.astype(BF)
    rest = value - high.astype(F32)
    mid = rest.astype(BF)
    return high, mid, (rest - mid.astype(F32)).astype(BF)


def total(left, right):
    return functools.reduce(operator.add, [x * y for x, y in zip(left, right)])


def invert2(m):
    scale = 1.0 / (m[0][0] * m[1][1] - m[0][1] * m[1][0])
    return [[m[1][1] * scale, -(m[0][1] * scale)], [-(m[1][0] * scale), m[0][0] * scale]]


def times2(x, y):
    return [[x[i][0] * y[0][j] + x[i][1] * y[1][j] for j in range(2)] for i in range(2)]


def factor4(p):
    block = lambda i, j: [[p[2 * i + r][2 * j + c] for c in range(2)] for r in range(2)]
    corner = invert2(block(0, 0))
    down = times2(block(1, 0), corner)
    across = times2(corner, block(0, 1))
    used = times2(block(1, 0), across)
    rest = block(1, 1)
    schur = invert2([[rest[i][j] - used[i][j] for j in range(2)] for i in range(2)])
    return corner, across, down, schur


def solve4(factors, r):
    corner, across, down, schur = factors
    left = [r[2 + i] - total(down[i], r[:2]) for i in range(2)]
    high = [total(corner[i], r[:2]) for i in range(2)]
    low = [total(schur[i], left) for i in range(2)]
    return [high[i] - total(across[i], low) for i in range(2)] + low


def solve_kernel(both, alpha, a_ref):
    width = alpha.shape[0]
    count = width // 8
    rows = both.shape[1]

    def tile(t):
        if rows >= 8:
            return both[t * 8 // rows, t * 8 % rows : t * 8 % rows + 8]
        return jnp.concatenate([both[t * (8 // rows) + k] for k in range(8 // rows)], axis=0)

    for t in range(count):
        alpha[8 * t : 8 * t + 8, :] = tile(t)
    curv = jnp.concatenate([tile(count + t) for t in range(count)], axis=0)
    a_ref[...] = (curv + curv.T) * 0.5
    spot = lax.broadcasted_iota(jnp.int32, (8, width), 0)
    part = lambda ref, t: ref[8 * t : 8 * t + 8, :]
    wide = lambda x, k: jnp.broadcast_to(x[:, k : k + 1], (8, width))
    for j in range(0, width, STEP):
        own, first = j // 8, j % 8
        row = lambda x, k: jnp.broadcast_to(x[first + k : first + k + 1, :], (8, width))
        a_own, g_own = part(a_ref, own), part(alpha, own)
        own_cols = [wide(a_own, j + k) for k in range(STEP)]
        factors = factor4([[row(own_cols[l], k) for l in range(STEP)] for k in range(STEP)])
        na = solve4(factors, [row(a_own, k) for k in range(STEP)])
        ng = solve4(factors, [row(g_own, k) for k in range(STEP)])

        def update(t, cols):
            ua = part(a_ref, t) - total(cols, na)
            ug = part(alpha, t) - total(cols, ng)
            if t == own:
                for k in range(STEP):
                    ua = jnp.where(spot == first + k, na[k], ua)
                    ug = jnp.where(spot == first + k, ng[k], ug)
            a_ref[8 * t : 8 * t + 8, :] = ua
            alpha[8 * t : 8 * t + 8, :] = ug

        ahead = (j + STEP) // 8
        early = [ahead] if ahead < count and ahead != own else []
        for t in early:
            update(t, [wide(part(a_ref, t), j + k) for k in range(STEP)])
        update(own, own_cols)
        others = [t for t in range(count) if t != own and t not in early]
        for g in range(0, len(others), GROUP):
            chosen = others[g : g + GROUP]
            cols = [[wide(part(a_ref, t), j + k) for t in chosen] for k in range(STEP)]
            for q, t in enumerate(chosen):
                update(t, [cols[k][q] for k in range(STEP)])


def finish_kernel(
    rows, r0, r1, r2, r3, gap, part0, term1, part1, term2, alpha, mult, resid, mult_v, resid_v, sems
):
    size = gap.shape[0]
    pieces = split3(alpha[...])
    down = lax.broadcasted_iota(jnp.int32, (TILE, r0.shape[0]), 0)
    moves = []
    for i in range(size // TILE):
        here = slice(i * TILE, (i + 1) * TILE)
        mult_v[here, :] = sum(mm(f, p) for p in pieces[::-1] for f in (term1[here, :], part1[here, :]))
        moves.append(pltpu.make_async_copy(mult_v.at[here, :], mult.at[here, :], sems.at[0, i]))
        moves[-1].start()
        got = None
        for d, r in enumerate((r0, r1, r2, r3)):
            hit = down + i * TILE == rows[0, 0, d : d + 1, :]
            piece = mm(jnp.where(hit, 1.0, 0.0).astype(BF), r[...])
            got = piece if got is None else got + piece
        got = got.astype(BF)
        step = sum(mm(f, p) for p in pieces[::-1] for f in (term2[here, :], got))
        resid_v[here, :] = gap[here, :].astype(F32) + part0[here, :].astype(F32) - step
        moves.append(pltpu.make_async_copy(resid_v.at[here, :], resid.at[here, :], sems.at[1, i]))
        moves[-1].start()
    for move in moves:
        move.wait()


def exchange(piece, sizes):
    span_count, chord_count = sizes
    up = lambda n: [(i, i + 1) for i in range(n - 1)]
    down = lambda n: [(i + 1, i) for i in range(n - 1)]
    return (
        lax.ppermute(piece[1], SPAN, up(span_count)),
        lax.ppermute(piece[0], SPAN, down(span_count)),
        lax.ppermute(piece[3], "y", up(chord_count)),
        lax.ppermute(piece[2], "y", down(chord_count)),
    )


def reduce_all(value):
    rows, width = value.shape
    plane = lax.axis_size(PLANE)
    height = lax.axis_size("z")
    chunks = lax.all_to_all(value.reshape(plane, rows // plane, width), PLANE, 0, 0)
    chunk = jnp.sum(chunks, axis=0)
    layers = lax.all_to_all(jnp.broadcast_to(chunk[None], (height,) + chunk.shape), "z", 0, 0)
    chunk = jnp.sum(layers, axis=0)
    return lax.all_to_all(jnp.broadcast_to(chunk[None], (plane,) + chunk.shape), PLANE, 0, 0)


def shards(sizes, disp, packed, fscale, dscale, diag, rows, signs, counts):
    size, width = disp.shape[2:]
    slots = rows.shape[3]
    disp, packed = disp[0, 0], packed[0, 0]
    field, square, piece = ((size, width), BF), ((size, size), BF), ((slots, width), BF)
    like = lambda x: (x.shape, x.dtype)
    pick, *out = call(
        pack_kernel,
        [square] + [piece] * 4 + [field] + [like(x) for x in (rows, disp, packed, diag, dscale, fscale)],
        [HB] * 8,
        [pltpu.VMEM(signs.shape, signs.dtype), pltpu.SMEM(counts.shape, counts.dtype), pltpu.SemaphoreType.DMA((8,))],
    )(*(pltpu.with_memory_space_constraint(x, pltpu.HBM) for x in (rows, signs, counts, disp, packed, diag, dscale, fscale)))
    live_sign, rows, disp, packed, diag, dscale, fscale = out[4:]
    got0 = exchange(out[:4], sizes)
    put, sign_row, gap, flex, diri = call(build_kernel, [square, field, field, square, square], [VM] * 5)(
        rows, live_sign, disp, packed, diag
    )

    def operate(block, scale, base, got):
        part, term, *sent = call(
            apply_kernel, [field] * 2 + [piece] * 4, [VM] * 10, [pltpu.VMEM((size, width), BF)], flops=8 * 10**8
        )(put, pick, block, sign_row, scale, base, *got)
        return part, term, sent

    def local_gram(base, partner, term):
        return call(gram_kernel, [((width, width), F32)], [VM] * 3)(base, partner, term)[0]

    part0, term1, sent = operate(diri, dscale, gap, got0)
    got1 = exchange(sent, sizes)
    gamma = local_gram(gap, part0, term1)
    part1, term2, sent = operate(flex, fscale, term1, got1)
    got2 = exchange(sent, sizes)
    curv = local_gram(term1, part1, term2)
    both = reduce_all(jnp.concatenate([gamma, curv], axis=0))
    alpha = call(solve_kernel, [((width, width), F32)], [VM], [pltpu.VMEM((width, width), F32)])(both)[0]
    whole = ((size, width), F32)
    mult, resid = call(
        finish_kernel,
        [whole] * 2,
        [VM] * 11,
        [pltpu.VMEM(*whole), pltpu.VMEM(*whole), pltpu.SemaphoreType.DMA((2, size // TILE))],
        out_spec=HB,
    )(rows, *got2, gap, part0, term1, part1, term2, alpha)
    return mult[None, None], resid[None, None]


def solution(mesh):
    span_count, chord_count = mesh.shape["span"], mesh.shape["chord"]
    grid = (span_count // (X_CHIPS * CORES), X_CHIPS, CORES, chord_count)
    fine = Mesh(mesh.devices.reshape(grid), SPAN + ("y",))
    spec = lambda extra: P(SPAN, "y", *([None] * extra))
    return jax.shard_map(
        functools.partial(shards, (span_count, chord_count)),
        mesh=fine,
        in_specs=tuple(spec(n) for n in (2, 2, 1, 1, 1, 2, 2, 1)),
        out_specs=(spec(2), spec(2)),
        check_vma=False,
    )
```
